32 devices in a mesh: fsdp: 8 (over z, y), tp: 4 (over x, core).
Axes of the slice: x: 2, y: 2, z: 4, core: 2. Of those that a mesh axis runs over, the one named last changes fastest.
Arguments:
- inputs: bfloat16 [4096, 1024], P(('fsdp', 'tp')), may hold values from -6 to 6
- cotangent: bfloat16 [4096, 1024], P(('fsdp', 'tp')), may hold values from -6 to 6
- lengths: int32 [8, 8], P('fsdp'), may hold values from 1 to 256, 512 in all within a row
- qkv_weight: bfloat16 [2, 3, 1024, 1024], P(None, None, 'fsdp', 'tp'), as said below
- qv_bias: bfloat16 [2, 2, 1024], P(None, None, ('tp', 'fsdp')), may hold values from -3 to 3
- out_weight: bfloat16 [2, 1024, 1024], P(None, 'tp', 'fsdp'), may hold values from -1 to 1
- fc_weight: bfloat16 [2, 1024, 4096], P(None, 'fsdp', 'tp'), may hold values from -0.1875 to 0.1875
- fc_bias: bfloat16 [2, 4096], P(None, ('tp', 'fsdp')), may hold values from -3 to 3
- proj_weight: bfloat16 [2, 4096, 1024], P(None, 'tp', 'fsdp'), may hold values from -0.09375 to 0.09375
- norm_gains: float32 [2, 2, 1024], P(None, None, ('fsdp', 'tp')), may hold values from 0.25 to 1.75
- shifts: float32 [2, 4, 1024], P(None, None, ('fsdp', 'tp')), may hold values from -3 to 3
Outputs:
- out_acts: bfloat16 [4096, 1024], P(('fsdp', 'tp'))
- in_grad: float32 [4096, 1024], P(('fsdp', 'tp'))
- qkv_grad: float32 [2, 3, 1024, 1024], P(None, None, 'fsdp', 'tp')
- qv_bias_grad: float32 [2, 2, 1024], P(None, None, ('tp', 'fsdp'))
- out_grad: float32 [2, 1024, 1024], P(None, 'tp', 'fsdp')
- fc_grad: float32 [2, 1024, 4096], P(None, 'fsdp', 'tp')
- fc_bias_grad: float32 [2, 4096], P(None, ('tp', 'fsdp'))
- proj_grad: float32 [2, 4096, 1024], P(None, 'tp', 'fsdp')
- gains_grad: float32 [2, 2, 1024], P(None, None, ('fsdp', 'tp'))
- shifts_grad: float32 [2, 4, 1024], P(None, None, ('fsdp', 'tp'))
The draws below stay inside these ranges and needn't reach their ends.
Inputs may be any that keep to these rules, and one draw needn't show every extreme that they name: Row g holds the lengths of group g's sequences in row order; they sum to 512 and the longest is 256. `qkv_weight`: columns h * 64 to (h + 1) * 64 - 1 of each projection belong to head h. Every entry lies between -6 / sqrt(1024) and 6 / sqrt(1024).
All inputs are finite; a program needn't handle non-finite values.
Results may differ from the reference program's by a relative error of at most 0.023.
Values may be sent and summed in bfloat16 or wider, within the bound.
No kernel may reach another device: no remote copies, remote signals or barrier semaphores. Data moves between devices by JAX's collectives and lax.ppermute only.
A program may use at most 128 MiB of HBM per device.

```python
import math
import jax
import jax.numpy as jnp
import numpy as np
from jax import lax

D = 1024
HEAD_DIM = 64
FF = 4096
LAYERS = 2
SLOTS = 8
TOK_GROUP = 512
SEQ_MAX = 256
TOKENS = 4096
N_FSDP = 8


def draw_qkv_weight(key, part):
    base = jax.random.normal(key, (LAYERS, 3, D, D), jnp.float32) * D ** (-0.5)
    base = jnp.clip(base, -6.0 * D ** (-0.5), 6.0 * D ** (-0.5))
    return base.astype(jnp.bfloat16)


def level_of(rng, shape, cuts, smallest, largest):
    gain = 1.0
    for dim, parts in cuts:
        steps = jax.random.uniform(jax.random.fold_in(jax.random.fold_in(rng, 6), dim), (parts,), jnp.float32, smallest / len(cuts), largest / len(cuts))
        gain = gain * jnp.repeat(jnp.exp(steps), shape[dim] // parts).reshape((-1,) + (1,) * (len(shape) - 1 - dim))
    return gain


def length_profile(amount, total, reach, skew):
    weights = [(1 << 20) // math.isqrt(grade ** skew) + 1 for grade in range(2, amount + 1)]
    rest, given = total - reach - (amount - 1), [1] * (amount - 1)
    while rest > 0:
        movable = [i for i in range(amount - 1) if given[i] < reach]
        whole, left = sum([weights[i] for i in movable]), rest
        for i in movable:
            extra = min(reach - given[i], max(1, left * weights[i] // whole), rest)
            given[i] = given[i] + extra
            rest = rest - extra
    return np.array([reach] + given)


def ragged_sizes(own_key, count, total, reach, slope):
    if count == 2:
        one = jax.random.randint(own_key, (), max(1, total - reach), min(reach, total - 1) + 1)
        return jnp.stack([one, total - one])
    sizes = jnp.asarray(length_profile(count, total, reach, slope), jnp.int32)
    twos = (count - 1) // 2
    source_of, taker = sizes[1:1 + 2 * twos:2], sizes[2:2 + 2 * twos:2]
    margin = jnp.minimum(source_of - 1, reach - taker)
    moved = jax.random.randint(jax.random.fold_in(own_key, 1), (twos,), 0, 1 << 20) % (margin + 1)
    sizes = sizes.at[1:1 + 2 * twos:2].set(source_of - moved).at[2:2 + 2 * twos:2].set(taker + moved)
    return sizes[jax.random.permutation(jax.random.fold_in(own_key, 2), count)]


def centred(stream_key, shape, deviation, reach, shards=(), kind=jnp.bfloat16):
    drawn = jax.random.normal(stream_key, shape, jnp.float32) * deviation
    if len(shards) > 0:
        drawn = level_of(stream_key, shape, shards, -0.22, 0.18) * drawn
    return jnp.clip(drawn, min=-reach, max=reach).astype(kind)


def setup_inputs(seed: int = 0) -> dict:
    streams_of = jax.random.split(jax.random.key(seed), 12)
    return {
        "inputs": centred(streams_of[0], (TOKENS, D), 1.0, 6.0, ((0, 32),)),
        "cotangent": centred(streams_of[1], (TOKENS, D), 1.0, 6.0, ((0, 32),)),
        "lengths": jax.vmap(lambda own: ragged_sizes(own, SLOTS, TOK_GROUP, SEQ_MAX, 2))(jax.random.split(streams_of[2], N_FSDP)).reshape((N_FSDP, SLOTS)).astype(jnp.int32),
        "qkv_weight": draw_qkv_weight(jax.random.fold_in(streams_of[11], 71), 0),
        "qv_bias": centred(streams_of[4], (LAYERS, 2, D), 0.5, 3.0, ((2, 32),)),
        "out_weight": centred(streams_of[5], (LAYERS, D, D), (D // 32) ** -0.5, 1.0, ((1, 4), (2, 8))),
        "fc_weight": centred(streams_of[6], (LAYERS, D, FF), D ** -0.5, 0.1875, ((1, 8), (2, 4))),
        "fc_bias": centred(streams_of[7], (LAYERS, FF), 0.5, 3.0, ((1, 32),)),
        "proj_weight": centred(streams_of[8], (LAYERS, FF, D), FF ** -0.5, 0.09375, ((1, 4), (2, 8))),
        "norm_gains": jnp.clip(1.0 + 0.15 * jax.random.normal(streams_of[9], (LAYERS, 2, D), jnp.float32), 0.25, 1.75),
        "shifts": centred(streams_of[10], (LAYERS, 4, D), 0.5, 3.0, ((2, 32),), jnp.float32),
    }


eps_norm = 1e-05

def to_low(values):
    return lax.optimization_barrier(values.astype(jnp.bfloat16))

def norm_stats(values):
    centre = values - lax.optimization_barrier(jnp.mean(values, axis=-1, keepdims=True))
    variance = lax.optimization_barrier(jnp.mean(centre * centre, axis=-1, keepdims=True))
    inv_std = lax.rsqrt(variance + eps_norm)
    return (centre * inv_std, inv_std)

def norm_back(d_normed, normed, inv_std):
    return inv_std * (d_normed - lax.optimization_barrier(jnp.mean(d_normed, axis=-1, keepdims=True)) - normed * lax.optimization_barrier(jnp.mean(d_normed * normed, axis=-1, keepdims=True)))

def gelu_tanh(values):
    return jax.nn.gelu(values, approximate=True)

def gelu_back(pre_act, d_act):
    return jax.vjp(gelu_tanh, pre_act)[1](d_act)[0]

def allowed_pairs(seq_lens, group_len):
    bounds = jnp.cumsum(seq_lens)
    positions = jnp.arange(group_len, dtype=jnp.int32)
    segment = lax.optimization_barrier(jnp.sum((positions[:, None] >= bounds[None, :]).astype(jnp.int32), axis=1))
    return (segment[:, None] == segment[None, :]) & (positions[None, :] <= positions[:, None])

def head_split(values):
    return values.reshape(values.shape[0], -1, HEAD_DIM).astype(jnp.float32)

def scores_of(queries, keys_in, allowed):
    raw = jnp.einsum('qhd,khd->hqk', head_split(queries), head_split(keys_in)) * HEAD_DIM ** (-0.5)
    return jnp.where(allowed[None], raw, -1e+30)

def attend(queries, keys_in, values_in, allowed):
    scores = scores_of(queries, keys_in, allowed)
    row_top = lax.optimization_barrier(jnp.max(scores, axis=-1))
    log_total = row_top + jnp.log(lax.optimization_barrier(jnp.sum(jnp.exp(scores - row_top[..., None]), axis=-1)))
    prob_low = to_low(jnp.exp(scores - log_total[..., None]))
    mixed_heads = jnp.einsum('hqk,khd->qhd', prob_low.astype(jnp.float32), head_split(values_in))
    return (to_low(mixed_heads.reshape(mixed_heads.shape[0], -1)), log_total)

def attend_back(queries, keys_in, values_in, mixed_heads, log_total, d_mixed, allowed):
    scores = scores_of(queries, keys_in, allowed)
    probs = jnp.exp(scores - log_total[..., None])
    prob_low = to_low(probs).astype(jnp.float32)
    dm_heads = head_split(d_mixed)
    d_values = jnp.einsum('hqk,qhd->khd', prob_low, dm_heads)
    d_probs = jnp.einsum('qhd,khd->hqk', dm_heads, head_split(values_in))
    row_dot = jnp.transpose(lax.optimization_barrier(jnp.sum(head_split(mixed_heads) * dm_heads, axis=-1)))
    d_scores = to_low(probs * (d_probs - row_dot[:, :, None])).astype(jnp.float32)
    scale = HEAD_DIM ** (-0.5)
    d_queries = jnp.einsum('hqk,khd->qhd', d_scores, head_split(keys_in)) * scale
    d_keys = jnp.einsum('hqk,qhd->khd', d_scores, head_split(queries)) * scale
    group_len = queries.shape[0]
    return (d_queries.reshape(group_len, -1), d_keys.reshape(group_len, -1), d_values.reshape(group_len, -1))

def group_pass(tokens, cot_rows, seq_lens, qkv_weight, qv_bias, out_weight, fc_weight, fc_bias, proj_weight, norm_gains, shifts):
    allowed = allowed_pairs(seq_lens, tokens.shape[0])
    residual = tokens.astype(jnp.float32)
    saved_acts = []
    for layer_id in range(LAYERS):
        norm_gain = norm_gains[layer_id]
        offset_rows = shifts[layer_id]
        normed_one, inv_one = norm_stats(residual)
        act_one = to_low(normed_one * norm_gain[0] + offset_rows[0])
        bias_rows = jnp.stack([qv_bias[layer_id, 0].astype(jnp.float32), jnp.zeros((D,), jnp.float32), qv_bias[layer_id, 1].astype(jnp.float32)])
        projected = jnp.einsum('gd,cdh->cgh', act_one.astype(jnp.float32), qkv_weight[layer_id].astype(jnp.float32)) + bias_rows[:, None, :]
        projected = to_low(projected)
        mixed_heads, log_total = attend(projected[0], projected[1], projected[2], allowed)
        middle = residual + jnp.dot(mixed_heads, out_weight[layer_id], preferred_element_type=jnp.float32) + offset_rows[2]
        normed_two, inv_two = norm_stats(middle)
        act_two = to_low(normed_two * norm_gain[1] + offset_rows[1])
        pre_act = jnp.dot(act_two, fc_weight[layer_id], preferred_element_type=jnp.float32) + fc_bias[layer_id].astype(jnp.float32)
        hidden = to_low(gelu_tanh(pre_act))
        after_block = middle + jnp.dot(hidden, proj_weight[layer_id], preferred_element_type=jnp.float32) + offset_rows[3]
        saved_acts.append((residual, act_one, projected, mixed_heads, log_total, middle, act_two, pre_act, hidden))
        residual = after_block
    out_rows = residual.astype(jnp.bfloat16)
    d_res = cot_rows.astype(jnp.float32)
    grad_lists = [[None] * LAYERS for member in range(8)]
    for layer_id in reversed(range(LAYERS)):
        residual, act_one, projected, mixed_heads, log_total, middle, act_two, pre_act, hidden = saved_acts[layer_id]
        norm_gain = norm_gains[layer_id]
        d_after = d_res
        d_low = to_low(d_after)
        d_proj = jnp.dot(hidden.T, d_low, preferred_element_type=jnp.float32)
        d_hidden = jnp.dot(d_low, proj_weight[layer_id].T, preferred_element_type=jnp.float32)
        d_pre = gelu_back(pre_act, d_hidden)
        d_pre_low = to_low(d_pre)
        d_fc = jnp.dot(act_two.T, d_pre_low, preferred_element_type=jnp.float32)
        d_fc_bias = lax.optimization_barrier(jnp.sum(d_pre, axis=0))
        d_act_two = jnp.dot(d_pre_low, fc_weight[layer_id].T, preferred_element_type=jnp.float32)
        normed_two, inv_two = norm_stats(middle)
        d_middle = d_after + norm_back(d_act_two * norm_gain[1], normed_two, inv_two)
        d_mid_low = to_low(d_middle)
        d_out = jnp.dot(mixed_heads.T, d_mid_low, preferred_element_type=jnp.float32)
        d_mixed = to_low(jnp.dot(d_mid_low, out_weight[layer_id].T, preferred_element_type=jnp.float32))
        d_queries, d_keys, d_values = attend_back(projected[0], projected[1], projected[2], mixed_heads, log_total, d_mixed, allowed)
        d_bias = jnp.stack([lax.optimization_barrier(jnp.sum(d_queries, axis=0)), lax.optimization_barrier(jnp.sum(d_values, axis=0))])
        d_proj_low = to_low(jnp.stack([d_queries, d_keys, d_values])).astype(jnp.float32)
        d_qkv = jnp.einsum('gd,cgh->cdh', act_one.astype(jnp.float32), d_proj_low)
        d_act_one = jnp.einsum('cgh,cdh->gd', d_proj_low, qkv_weight[layer_id].astype(jnp.float32))
        normed_one, inv_one = norm_stats(residual)
        d_res = d_middle + norm_back(d_act_one * norm_gain[0], normed_one, inv_one)
        gain_rows = jnp.stack([lax.optimization_barrier(jnp.sum(d_act_one * normed_one, axis=0)), lax.optimization_barrier(jnp.sum(d_act_two * normed_two, axis=0))])
        shift_rows = jnp.stack([lax.optimization_barrier(jnp.sum(d_act_one, axis=0)), lax.optimization_barrier(jnp.sum(d_act_two, axis=0)), lax.optimization_barrier(jnp.sum(d_middle, axis=0)), lax.optimization_barrier(jnp.sum(d_after, axis=0))])
        layer_grads = (d_qkv, d_bias, d_out, d_fc, d_fc_bias, d_proj, gain_rows, shift_rows)
        for member in range(8):
            grad_lists[member][layer_id] = layer_grads[member]
    stacked = tuple((jnp.stack(grad_lists[member]) for member in range(8)))
    return (out_rows, d_res, stacked)

def reference(inputs, cotangent, lengths, qkv_weight, qv_bias, out_weight, fc_weight, fc_bias, proj_weight, norm_gains, shifts):

    def visit_group(totals, pieces):
        tokens, cot_rows, seq_lens = pieces
        out_rows, d_rows, grads = group_pass(tokens, cot_rows, seq_lens, qkv_weight, qv_bias, out_weight, fc_weight, fc_bias, proj_weight, norm_gains, shifts)
        return (tuple((totals[member] + grads[member] for member in range(8))), (out_rows, d_rows))
    zeros = (jnp.zeros((LAYERS, 3, D, D), jnp.float32), jnp.zeros((LAYERS, 2, D), jnp.float32), jnp.zeros((LAYERS, D, D), jnp.float32), jnp.zeros((LAYERS, D, FF), jnp.float32), jnp.zeros((LAYERS, FF), jnp.float32), jnp.zeros((LAYERS, FF, D), jnp.float32), jnp.zeros((LAYERS, 2, D), jnp.float32), jnp.zeros((LAYERS, 4, D), jnp.float32))
    totals, (out_all, d_all) = lax.scan(visit_group, zeros, (inputs.reshape(N_FSDP, TOK_GROUP, D), cotangent.reshape(N_FSDP, TOK_GROUP, D), lengths))
    return (out_all.reshape(TOKENS, D), d_all.reshape(TOKENS, D), totals[0], totals[1], totals[2], totals[3], totals[4], totals[5], totals[6], totals[7])
```

```python
import jax
import jax.numpy as jnp
from jax import lax
from jax.sharding import PartitionSpec as P

HEAD_DIM = 64
LAYERS = 2


eps_norm = 1e-05


def norm_stats(values):
    centre = values - jnp.mean(values, axis=-1, keepdims=True)
    variance = jnp.mean(centre * centre, axis=-1, keepdims=True)
    inv_std = lax.rsqrt(variance + eps_norm)
    return (centre * inv_std, inv_std)


def norm_back(d_normed, normed, inv_std):
    return inv_std * (
        d_normed
        - jnp.mean(d_normed, axis=-1, keepdims=True)
        - normed * jnp.mean(d_normed * normed, axis=-1, keepdims=True)
    )


def gelu_tanh(values):
    return jax.nn.gelu(values, approximate=True)


def gelu_back(pre_act, d_act):
    return jax.vjp(gelu_tanh, pre_act)[1](d_act)[0]


def xor_permute(values, axis, mask):
    count = lax.axis_size(axis)
    return lax.ppermute(values, axis, [(src, src ^ mask) for src in range(count)])


def butterfly_sum(values, axis):
    mask = 1
    while mask < lax.axis_size(axis):
        values = values + xor_permute(values, axis, mask)
        mask *= 2
    return values


def owner_order():
    place = lax.axis_index("tp")
    return [place, place ^ 2, place ^ 1, place ^ 3]


def gather_rows(values):
    pair = jnp.concatenate([values, xor_permute(values, "tp", 2)], axis=0)
    return jnp.concatenate([pair, xor_permute(pair, "tp", 1)], axis=0)


def sum_rows(partial_fn, tok_rows):
    far = partial_fn(slice(2 * tok_rows, 4 * tok_rows)).astype(jnp.bfloat16)
    got = xor_permute(far, "tp", 1).astype(jnp.float32)
    near = partial_fn(slice(0, 2 * tok_rows)) + got
    across = xor_permute(near[tok_rows:].astype(jnp.bfloat16), "tp", 2).astype(jnp.float32)
    return near[:tok_rows] + across


def allowed_pairs(seq_lens, tok_rows):
    bounds = jnp.cumsum(seq_lens)
    rows = jnp.arange(tok_rows, dtype=jnp.int32)
    positions = jnp.concatenate([owner * tok_rows + rows for owner in owner_order()])
    segment = jnp.sum((positions[:, None] >= bounds[None, :]).astype(jnp.int32), axis=1)
    return (segment[:, None] == segment[None, :]) & (positions[None, :] <= positions[:, None])


def one_hot_columns(count, width, first):
    return (
        lax.broadcasted_iota(jnp.int32, (count, width), 1)
        == lax.broadcasted_iota(jnp.int32, (count, width), 0) + first
    ).astype(jnp.float32)


def place_columns(values, width, first):
    return jnp.dot(
        values,
        one_hot_columns(values.shape[1], width, first),
        precision=lax.Precision.HIGHEST,
        preferred_element_type=jnp.float32,
    )


def take_columns(values, count, first):
    return lax.dot_general(
        values,
        one_hot_columns(count, values.shape[1], first),
        (((1,), (1,)), ((), ())),
        precision=lax.Precision.HIGHEST,
        preferred_element_type=jnp.float32,
    )


def head_split(values):
    return values.reshape(values.shape[0], -1, HEAD_DIM)


def scores_of(queries, keys_in, allowed):
    raw = jnp.einsum(
        "qhd,khd->hqk", head_split(queries), head_split(keys_in), preferred_element_type=jnp.float32
    ) * HEAD_DIM ** (-0.5)
    return jnp.where(allowed[None], raw, -1e30)


def attend(queries, keys_in, values_in, allowed):
    scores = scores_of(queries, keys_in, allowed)
    row_top = jnp.max(scores, axis=-1)
    log_total = row_top + jnp.log(jnp.sum(jnp.exp(scores - row_top[..., None]), axis=-1))
    prob_low = jnp.exp(scores - log_total[..., None]).astype(jnp.bfloat16)
    mixed_heads = jnp.einsum(
        "hqk,khd->qhd", prob_low, head_split(values_in), preferred_element_type=jnp.float32
    )
    return (mixed_heads.reshape(mixed_heads.shape[0], -1).astype(jnp.bfloat16), log_total)


def attend_back(queries, keys_in, values_in, mixed_heads, log_total, d_mixed, allowed):
    scores = scores_of(queries, keys_in, allowed)
    probs = jnp.exp(scores - log_total[..., None])
    prob_low = probs.astype(jnp.bfloat16)
    dm_heads = head_split(d_mixed)
    d_values = jnp.einsum("hqk,qhd->khd", prob_low, dm_heads, preferred_element_type=jnp.float32)
    d_probs = jnp.einsum(
        "qhd,khd->hqk", dm_heads, head_split(values_in), preferred_element_type=jnp.float32
    )
    row_dot = jnp.transpose(
        jnp.sum(head_split(mixed_heads).astype(jnp.float32) * dm_heads.astype(jnp.float32), axis=-1)
    )
    d_scores = (probs * (d_probs - row_dot[:, :, None])).astype(jnp.bfloat16)
    scale = HEAD_DIM ** (-0.5)
    d_queries = (
        jnp.einsum(
            "hqk,khd->qhd", d_scores, head_split(keys_in), preferred_element_type=jnp.float32
        )
        * scale
    )
    d_keys = (
        jnp.einsum(
            "hqk,qhd->khd", d_scores, head_split(queries), preferred_element_type=jnp.float32
        )
        * scale
    )
    group_len = queries.shape[0]
    return (
        d_queries.reshape(group_len, -1),
        d_keys.reshape(group_len, -1),
        d_values.reshape(group_len, -1),
    )


def contract_first(left, right):
    return lax.dot_general(
        left, right, (((0,), (0,)), ((), ())), preferred_element_type=jnp.float32
    )


def contract_last(left, right):
    return lax.dot_general(
        left, right, (((1,), (1,)), ((), ())), preferred_element_type=jnp.float32
    )


def pack_layer(qkv_weight, out_weight, fc_weight, proj_weight):
    rows = fc_weight.shape[0]
    return [
        jnp.transpose(qkv_weight, (1, 0, 2)).reshape(rows, -1),
        jnp.transpose(out_weight),
        fc_weight,
        jnp.transpose(proj_weight),
    ]


def gather_weights(parts):
    return lax.all_gather(jnp.concatenate(parts, axis=1), "fsdp", axis=0, tiled=True)


def scatter_grads(parts):
    packed = jnp.concatenate([part.astype(jnp.bfloat16) for part in parts], axis=1)
    return lax.psum_scatter(packed, "fsdp", scatter_dimension=0, tiled=True).astype(jnp.float32)


def body(
    inputs,
    cotangent,
    lengths,
    qkv_weight,
    qv_bias,
    out_weight,
    fc_weight,
    fc_bias,
    proj_weight,
    norm_gains,
    shifts,
):
    tok_rows, width = inputs.shape
    fsdp_place = lax.axis_index("fsdp")
    device_place = fsdp_place * lax.axis_size("tp") + lax.axis_index("tp")
    heads_width = qkv_weight.shape[3]
    units = fc_weight.shape[2]
    gain_cols = norm_gains.shape[2]
    bias_cols = qv_bias.shape[2]
    unit_cols = fc_bias.shape[1]

    packed = [
        pack_layer(qkv_weight[layer], out_weight[layer], fc_weight[layer], proj_weight[layer])
        for layer in range(LAYERS)
    ]
    qkv_all = [None] * LAYERS
    rest_all = [None] * LAYERS
    qkv_all[0] = gather_weights(packed[0][:1])
    rest_all[0] = gather_weights(packed[0][1:])
    both = gather_weights(packed[1])
    qkv_all[1] = both[:, : 3 * heads_width]
    rest_all[1] = both[:, 3 * heads_width :]

    norm_rows = jnp.concatenate(
        [norm_gains.reshape(-1, gain_cols), shifts.reshape(-1, gain_cols)], axis=0
    )
    norm_count = norm_rows.shape[0]
    small = jnp.concatenate(
        [
            place_columns(norm_rows, width, device_place * gain_cols),
            place_columns(
                qv_bias.reshape(-1, bias_cols).astype(jnp.float32), width, fsdp_place * bias_cols
            ),
            place_columns(fc_bias.astype(jnp.float32), units, fsdp_place * unit_cols),
        ],
        axis=0,
    )
    small = butterfly_sum(small, "fsdp")
    norm_all = butterfly_sum(small[:norm_count], "tp")
    gains_all = norm_all[: 2 * LAYERS].reshape(LAYERS, 2, width)
    shifts_all = norm_all[2 * LAYERS :].reshape(LAYERS, 4, width)
    qv_all = small[norm_count : norm_count + 2 * LAYERS, :heads_width].reshape(
        LAYERS, 2, heads_width
    )
    fc_bias_all = small[norm_count + 2 * LAYERS :]

    allowed = allowed_pairs(lengths[0], tok_rows)
    residual = inputs.astype(jnp.float32)
    saved_acts = []
    weights = []
    for layer_id in range(LAYERS):
        w_qkv = qkv_all[layer_id]
        rest = rest_all[layer_id]
        w_out_t = rest[:, :heads_width]
        w_fc = rest[:, heads_width : heads_width + units]
        w_proj_t = rest[:, heads_width + units :]
        weights.append((w_qkv, w_out_t, w_fc, w_proj_t))
        norm_gain = gains_all[layer_id]
        offset_rows = shifts_all[layer_id]
        normed_one, inv_one = norm_stats(residual)
        act_one = gather_rows((normed_one * norm_gain[0] + offset_rows[0]).astype(jnp.bfloat16))
        bias_row = jnp.concatenate(
            [qv_all[layer_id, 0], jnp.zeros((heads_width,), jnp.float32), qv_all[layer_id, 1]]
        )
        projected = (
            jnp.dot(act_one, w_qkv, preferred_element_type=jnp.float32) + bias_row
        ).astype(jnp.bfloat16)
        projected = [
            projected[:, part * heads_width : (part + 1) * heads_width] for part in range(3)
        ]
        mixed_heads, log_total = attend(projected[0], projected[1], projected[2], allowed)

        def out_part(rows, mixed_heads=mixed_heads, w_out_t=w_out_t):
            return contract_last(mixed_heads[rows], w_out_t)

        middle = residual + sum_rows(out_part, tok_rows) + offset_rows[2]
        normed_two, inv_two = norm_stats(middle)
        act_two = gather_rows((normed_two * norm_gain[1] + offset_rows[1]).astype(jnp.bfloat16))
        pre_act = jnp.dot(act_two, w_fc, preferred_element_type=jnp.float32) + fc_bias_all[layer_id]
        hidden = gelu_tanh(pre_act).astype(jnp.bfloat16)

        def mlp_part(rows, hidden=hidden, w_proj_t=w_proj_t):
            return contract_last(hidden[rows], w_proj_t)

        after_block = middle + sum_rows(mlp_part, tok_rows) + offset_rows[3]
        saved_acts.append(
            (residual, act_one, projected, mixed_heads, log_total, middle, act_two, pre_act, hidden)
        )
        residual = after_block
    out_rows = residual.astype(jnp.bfloat16)
    d_res = cotangent.astype(jnp.float32)
    gain_list = [None] * LAYERS
    shift_list = [None] * LAYERS
    qv_list = [None] * LAYERS
    fcb_list = [None] * LAYERS
    mlp_grads = [None] * LAYERS
    att_grads = [None] * LAYERS
    for layer_id in reversed(range(LAYERS)):
        w_qkv, w_out_t, w_fc, w_proj_t = weights[layer_id]
        norm_gain = gains_all[layer_id]
        residual, act_one, projected, mixed_heads, log_total, middle, act_two, pre_act, hidden = (
            saved_acts[layer_id]
        )
        d_after = d_res
        d_low = gather_rows(d_after.astype(jnp.bfloat16))
        d_proj_t = contract_first(d_low, hidden)
        d_hidden = jnp.dot(d_low, w_proj_t, preferred_element_type=jnp.float32)
        d_pre = gelu_back(pre_act, d_hidden)
        d_pre_low = d_pre.astype(jnp.bfloat16)
        d_fc = contract_first(act_two, d_pre_low)
        fcb_list[layer_id] = jnp.sum(d_pre, axis=0)
        mlp_grads[layer_id] = scatter_grads([d_fc, d_proj_t])

        def fc_part(rows, d_pre_low=d_pre_low, w_fc=w_fc):
            return contract_last(d_pre_low[rows], w_fc)

        d_act_two = sum_rows(fc_part, tok_rows)
        normed_two, inv_two = norm_stats(middle)
        d_middle = d_after + norm_back(d_act_two * norm_gain[1], normed_two, inv_two)
        d_mid_low = gather_rows(d_middle.astype(jnp.bfloat16))
        d_out_t = contract_first(d_mid_low, mixed_heads)
        d_mixed = jnp.dot(d_mid_low, w_out_t, preferred_element_type=jnp.float32).astype(
            jnp.bfloat16
        )
        d_queries, d_keys, d_values = attend_back(
            projected[0], projected[1], projected[2], mixed_heads, log_total, d_mixed, allowed
        )
        qv_list[layer_id] = jnp.stack([jnp.sum(d_queries, axis=0), jnp.sum(d_values, axis=0)])
        d_proj_low = jnp.concatenate([d_queries, d_keys, d_values], axis=1).astype(jnp.bfloat16)
        d_qkv = contract_first(act_one, d_proj_low)
        att_grads[layer_id] = scatter_grads([d_qkv, d_out_t])

        def qkv_part(rows, d_proj_low=d_proj_low, w_qkv=w_qkv):
            return contract_last(d_proj_low[rows], w_qkv)

        d_act_one = sum_rows(qkv_part, tok_rows)
        normed_one, inv_one = norm_stats(residual)
        d_res = d_middle + norm_back(d_act_one * norm_gain[0], normed_one, inv_one)
        gain_list[layer_id] = jnp.stack(
            [jnp.sum(d_act_one * normed_one, axis=0), jnp.sum(d_act_two * normed_two, axis=0)]
        )
        shift_list[layer_id] = jnp.stack(
            [
                jnp.sum(d_act_one, axis=0),
                jnp.sum(d_act_two, axis=0),
                jnp.sum(d_middle, axis=0),
                jnp.sum(d_after, axis=0),
            ]
        )
    qv_rows = jnp.concatenate(qv_list, axis=0)
    small = jnp.concatenate(
        gain_list
        + shift_list
        + [jnp.pad(qv_rows, ((0, 0), (0, width - heads_width))), jnp.stack(fcb_list)],
        axis=0,
    )
    small = butterfly_sum(small, "fsdp")
    norm_sum = take_columns(
        butterfly_sum(small[:norm_count], "tp"), gain_cols, device_place * gain_cols
    )
    qv_sum = take_columns(
        small[norm_count : norm_count + 2 * LAYERS, :heads_width], bias_cols, fsdp_place * bias_cols
    )
    fcb_sum = take_columns(small[norm_count + 2 * LAYERS :], unit_cols, fsdp_place * unit_cols)

    def layers_of(grads, columns):
        return [grads[layer][:, columns] for layer in range(LAYERS)]

    rows = fc_weight.shape[1]
    qkv_grad = jnp.stack(
        [
            jnp.transpose(part.reshape(rows, 3, heads_width), (1, 0, 2))
            for part in layers_of(att_grads, slice(0, 3 * heads_width))
        ]
    )
    out_grad = jnp.stack(
        [jnp.transpose(part) for part in layers_of(att_grads, slice(3 * heads_width, None))]
    )
    fc_grad = jnp.stack(layers_of(mlp_grads, slice(0, units)))
    proj_grad = jnp.stack([jnp.transpose(part) for part in layers_of(mlp_grads, slice(units, None))])
    return (
        out_rows,
        d_res,
        qkv_grad,
        qv_sum.reshape(LAYERS, 2, bias_cols),
        out_grad,
        fc_grad,
        fcb_sum,
        proj_grad,
        norm_sum[: 2 * LAYERS].reshape(LAYERS, 2, gain_cols),
        norm_sum[2 * LAYERS :].reshape(LAYERS, 4, gain_cols),
    )


def solution(mesh):
    in_specs = (
        P(("fsdp", "tp"), None),
        P(("fsdp", "tp"), None),
        P("fsdp", None),
        P(None, None, "fsdp", "tp"),
        P(None, None, ("tp", "fsdp")),
        P(None, "tp", "fsdp"),
        P(None, "fsdp", "tp"),
        P(None, ("tp", "fsdp")),
        P(None, "tp", "fsdp"),
        P(None, None, ("fsdp", "tp")),
        P(None, None, ("fsdp", "tp")),
    )
    out_specs = (
        P(("fsdp", "tp"), None),
        P(("fsdp", "tp"), None),
        P(None, None, "fsdp", "tp"),
        P(None, None, ("tp", "fsdp")),
        P(None, "tp", "fsdp"),
        P(None, "fsdp", "tp"),
        P(None, ("tp", "fsdp")),
        P(None, "tp", "fsdp"),
        P(None, None, ("fsdp", "tp")),
        P(None, None, ("fsdp", "tp")),
    )
    return jax.shard_map(body, mesh=mesh, in_specs=in_specs, out_specs=out_specs, check_vma=False)
```

```python
import jax
import jax.numpy as jnp
from jax import lax
from jax.sharding import PartitionSpec as P

HEAD_DIM = 64
LAYERS = 2


eps_norm = 1e-05


def norm_stats(values):
    centre = values - jnp.mean(values, axis=-1, keepdims=True)
    variance = jnp.mean(centre * centre, axis=-1, keepdims=True)
    inv_std = lax.rsqrt(variance + eps_norm)
    return (centre * inv_std, inv_std)


def norm_back(d_normed, normed, inv_std):
    return inv_std * (
        d_normed
        - jnp.mean(d_normed, axis=-1, keepdims=True)
        - normed * jnp.mean(d_normed * normed, axis=-1, keepdims=True)
    )


def gelu_tanh(values):
    return jax.nn.gelu(values, approximate=True)


def gelu_back(pre_act, d_act):
    return jax.vjp(gelu_tanh, pre_act)[1](d_act)[0]


def xor_permute(values, axis, mask):
    count = lax.axis_size(axis)
    return lax.ppermute(values, axis, [(src, src ^ mask) for src in range(count)])


def butterfly_sum(values, axis):
    mask = 1
    while mask < lax.axis_size(axis):
        values = values + xor_permute(values, axis, mask)
        mask *= 2
    return values


def owner_order():
    place = lax.axis_index("tp")
    return [place, place ^ 2, place ^ 1, place ^ 3]


def gather_rows(values):
    pair = jnp.concatenate([values, xor_permute(values, "tp", 2)], axis=0)
    return jnp.concatenate([pair, xor_permute(pair, "tp", 1)], axis=0)


def sum_rows(partial_fn, tok_rows):
    far = partial_fn(slice(2 * tok_rows, 4 * tok_rows)).astype(jnp.bfloat16)
    got = xor_permute(far, "tp", 1).astype(jnp.float32)
    near = partial_fn(slice(0, 2 * tok_rows)) + got
    across = xor_permute(near[tok_rows:].astype(jnp.bfloat16), "tp", 2).astype(jnp.float32)
    return near[:tok_rows] + across


def allowed_pairs(seq_lens, tok_rows):
    bounds = jnp.cumsum(seq_lens)
    rows = jnp.arange(tok_rows, dtype=jnp.int32)
    positions = jnp.concatenate([owner * tok_rows + rows for owner in owner_order()])
    segment = jnp.sum((positions[:, None] >= bounds[None, :]).astype(jnp.int32), axis=1)
    return (segment[:, None] == segment[None, :]) & (positions[None, :] <= positions[:, None])


def one_hot_columns(count, width, first):
    return (
        lax.broadcasted_iota(jnp.int32, (count, width), 1)
        == lax.broadcasted_iota(jnp.int32, (count, width), 0) + first
    ).astype(jnp.float32)


def place_columns(values, width, first):
    return jnp.dot(
        values,
        one_hot_columns(values.shape[1], width, first),
        precision=lax.Precision.HIGHEST,
        preferred_element_type=jnp.float32,
    )


def take_columns(values, count, first):
    return lax.dot_general(
        values,
        one_hot_columns(count, values.shape[1], first),
        (((1,), (1,)), ((), ())),
        precision=lax.Precision.HIGHEST,
        preferred_element_type=jnp.float32,
    )


def head_split(values):
    return values.reshape(values.shape[0], -1, HEAD_DIM)


def scores_of(queries, keys_in, allowed):
    raw = jnp.einsum(
        "qhd,khd->hqk", head_split(queries), head_split(keys_in), preferred_element_type=jnp.float32
    ) * HEAD_DIM ** (-0.5)
    return jnp.where(allowed[None], raw, -1e30)


def attend(queries, keys_in, values_in, allowed):
    scores = scores_of(queries, keys_in, allowed)
    row_top = jnp.max(scores, axis=-1)
    log_total = row_top + jnp.log(jnp.sum(jnp.exp(scores - row_top[..., None]), axis=-1))
    prob_low = jnp.exp(scores - log_total[..., None]).astype(jnp.bfloat16)
    mixed_heads = jnp.einsum(
        "hqk,khd->qhd", prob_low, head_split(values_in), preferred_element_type=jnp.float32
    )
    return (mixed_heads.reshape(mixed_heads.shape[0], -1).astype(jnp.bfloat16), log_total)


def attend_back(queries, keys_in, values_in, mixed_heads, log_total, d_mixed, allowed):
    scores = scores_of(queries, keys_in, allowed)
    probs = jnp.exp(scores - log_total[..., None])
    prob_low = probs.astype(jnp.bfloat16)
    dm_heads = head_split(d_mixed)
    d_values = jnp.einsum("hqk,qhd->khd", prob_low, dm_heads, preferred_element_type=jnp.float32)
    d_probs = jnp.einsum(
        "qhd,khd->hqk", dm_heads, head_split(values_in), preferred_element_type=jnp.float32
    )
    row_dot = jnp.transpose(
        jnp.sum(head_split(mixed_heads).astype(jnp.float32) * dm_heads.astype(jnp.float32), axis=-1)
    )
    d_scores = (probs * (d_probs - row_dot[:, :, None])).astype(jnp.bfloat16)
    scale = HEAD_DIM ** (-0.5)
    d_queries = (
        jnp.einsum(
            "hqk,khd->qhd", d_scores, head_split(keys_in), preferred_element_type=jnp.float32
        )
        * scale
    )
    d_keys = (
        jnp.einsum(
            "hqk,qhd->khd", d_scores, head_split(queries), preferred_element_type=jnp.float32
        )
        * scale
    )
    group_len = queries.shape[0]
    return (
        d_queries.reshape(group_len, -1),
        d_keys.reshape(group_len, -1),
        d_values.reshape(group_len, -1),
    )


def contract_first(left, right):
    return lax.dot_general(
        left, right, (((0,), (0,)), ((), ())), preferred_element_type=jnp.float32
    )


def contract_last(left, right):
    return lax.dot_general(
        left, right, (((1,), (1,)), ((), ())), preferred_element_type=jnp.float32
    )


def fsdp_stages():
    high = lax.axis_size("fsdp").bit_length() - 1
    stages = []
    while high > 0:
        low = max(high - 2, 0)
        stages.append([step << low for step in range(1, 1 << (high - low))])
        high = low
    return stages


def block_order():
    order = [0]
    for stage in fsdp_stages():
        order = order + [mask ^ member for mask in stage for member in order]
    return order


def own_order_matrix(width):
    size = width // lax.axis_size("fsdp")
    column = jnp.arange(width, dtype=jnp.int32)
    order = jnp.repeat(jnp.array(block_order(), jnp.int32), size)
    source = (lax.axis_index("fsdp") ^ order) * size + column % size
    return column[:, None] == source[None, :]


def move_columns(values, matrix, back=False):
    exact = values.dtype == jnp.bfloat16
    return lax.dot_general(
        values,
        matrix.astype(values.dtype),
        (((1,), (1 if back else 0,)), ((), ())),
        precision=lax.Precision.DEFAULT if exact else lax.Precision.HIGHEST,
        preferred_element_type=jnp.float32,
    ).astype(values.dtype)


def pack_layer(qkv_weight, out_weight, fc_weight, proj_weight):
    rows = fc_weight.shape[0]
    return [
        jnp.transpose(qkv_weight, (1, 0, 2)).reshape(rows, -1),
        jnp.transpose(out_weight),
        fc_weight,
        jnp.transpose(proj_weight),
    ]


def gather_chunks(chunks):
    held = list(chunks)
    for stage in fsdp_stages():
        for number, chunk in enumerate(held):
            if number:
                chunk, held[number - 1] = lax.optimization_barrier((chunk, held[number - 1]))
            held[number] = jnp.concatenate(
                [chunk] + [xor_permute(chunk, "fsdp", mask) for mask in stage], axis=0
            )
    return held


def scatter_grads(acts_and_grads):
    def partial(rows):
        return jnp.concatenate(
            [
                contract_first(act[:, rows], grad).astype(jnp.bfloat16)
                for act, grad in acts_and_grads
            ],
            axis=1,
        )

    width = acts_and_grads[0][0].shape[1]
    held = None
    for stage in reversed(fsdp_stages()):
        part = width // (len(stage) + 1)
        if held is None:
            send = [partial(slice(part * (k + 1), part * (k + 2))) for k in range(len(stage))]
            got = [xor_permute(piece, "fsdp", mask) for piece, mask in zip(send, stage)]
            total = partial(slice(0, part)).astype(jnp.float32)
        else:
            low = held.astype(jnp.bfloat16)
            got = [
                xor_permute(low[part * (k + 1) : part * (k + 2)], "fsdp", mask)
                for k, mask in enumerate(stage)
            ]
            total = held[:part]
        for piece in got:
            total = total + piece.astype(jnp.float32)
        held = total
        width = part
    return held


def body(
    inputs,
    cotangent,
    lengths,
    qkv_weight,
    qv_bias,
    out_weight,
    fc_weight,
    fc_bias,
    proj_weight,
    norm_gains,
    shifts,
):
    tok_rows, width = inputs.shape
    matrix = own_order_matrix(width)
    fsdp_place = lax.axis_index("fsdp")
    device_place = fsdp_place * lax.axis_size("tp") + lax.axis_index("tp")
    heads_width = qkv_weight.shape[3]
    units = fc_weight.shape[2]
    gain_cols = norm_gains.shape[2]
    bias_cols = qv_bias.shape[2]
    unit_cols = fc_bias.shape[1]

    packed = [
        pack_layer(qkv_weight[layer], out_weight[layer], fc_weight[layer], proj_weight[layer])
        for layer in range(LAYERS)
    ]
    chunks = []
    for w_qkv, w_out_t, w_fc, w_proj_t in packed:
        chunks += [w_qkv, jnp.concatenate([w_out_t, w_fc], axis=1), w_proj_t]
    chunks = gather_chunks(chunks)

    norm_rows = jnp.concatenate(
        [norm_gains.reshape(-1, gain_cols), shifts.reshape(-1, gain_cols)], axis=0
    )
    norm_count = norm_rows.shape[0]
    small = jnp.concatenate(
        [
            place_columns(norm_rows, width, device_place * gain_cols),
            place_columns(
                qv_bias.reshape(-1, bias_cols).astype(jnp.float32), width, fsdp_place * bias_cols
            ),
            place_columns(fc_bias.astype(jnp.float32), units, fsdp_place * unit_cols),
        ],
        axis=0,
    )
    small = butterfly_sum(small, "fsdp")
    norm_all = move_columns(butterfly_sum(small[:norm_count], "tp"), matrix)
    gains_all = norm_all[: 2 * LAYERS].reshape(LAYERS, 2, width)
    shifts_all = norm_all[2 * LAYERS :].reshape(LAYERS, 4, width)
    qv_all = small[norm_count : norm_count + 2 * LAYERS, :heads_width].reshape(
        LAYERS, 2, heads_width
    )
    fc_bias_all = small[norm_count + 2 * LAYERS :]

    allowed = allowed_pairs(lengths[0], tok_rows)
    both = move_columns(jnp.concatenate([inputs, cotangent], axis=0), matrix).astype(jnp.float32)
    residual = both[:tok_rows]
    saved_acts = []
    weights = []
    for layer_id in range(LAYERS):
        w_qkv, out_fc, w_proj_t = chunks[3 * layer_id : 3 * layer_id + 3]
        w_out_t = out_fc[:, :heads_width]
        w_fc = out_fc[:, heads_width:]
        weights.append((w_qkv, w_out_t, w_fc, w_proj_t))
        norm_gain = gains_all[layer_id]
        offset_rows = shifts_all[layer_id]
        normed_one, inv_one = norm_stats(residual)
        act_one = gather_rows((normed_one * norm_gain[0] + offset_rows[0]).astype(jnp.bfloat16))
        bias_row = jnp.concatenate(
            [qv_all[layer_id, 0], jnp.zeros((heads_width,), jnp.float32), qv_all[layer_id, 1]]
        )
        projected = (
            jnp.dot(act_one, w_qkv, preferred_element_type=jnp.float32) + bias_row
        ).astype(jnp.bfloat16)
        projected = [
            projected[:, part * heads_width : (part + 1) * heads_width] for part in range(3)
        ]
        mixed_heads, log_total = attend(projected[0], projected[1], projected[2], allowed)

        def out_part(rows, mixed_heads=mixed_heads, w_out_t=w_out_t):
            return contract_last(mixed_heads[rows], w_out_t)

        middle = residual + sum_rows(out_part, tok_rows) + offset_rows[2]
        normed_two, inv_two = norm_stats(middle)
        act_two = gather_rows((normed_two * norm_gain[1] + offset_rows[1]).astype(jnp.bfloat16))
        pre_act = jnp.dot(act_two, w_fc, preferred_element_type=jnp.float32) + fc_bias_all[layer_id]
        hidden = gelu_tanh(pre_act).astype(jnp.bfloat16)

        def mlp_part(rows, hidden=hidden, w_proj_t=w_proj_t):
            return contract_last(hidden[rows], w_proj_t)

        after_block = middle + sum_rows(mlp_part, tok_rows) + offset_rows[3]
        saved_acts.append(
            (residual, act_one, projected, mixed_heads, log_total, middle, act_two, pre_act, hidden)
        )
        residual = after_block
    out_rows = move_columns(residual.astype(jnp.bfloat16), matrix, back=True)
    d_res = both[tok_rows:]
    gain_list = [None] * LAYERS
    shift_list = [None] * LAYERS
    qv_list = [None] * LAYERS
    fcb_list = [None] * LAYERS
    fc_grads = [None] * LAYERS
    proj_grads = [None] * LAYERS
    att_grads = [None] * LAYERS
    for layer_id in reversed(range(LAYERS)):
        w_qkv, w_out_t, w_fc, w_proj_t = weights[layer_id]
        norm_gain = gains_all[layer_id]
        residual, act_one, projected, mixed_heads, log_total, middle, act_two, pre_act, hidden = (
            saved_acts[layer_id]
        )
        d_after = d_res
        d_low = gather_rows(d_after.astype(jnp.bfloat16))
        proj_grads[layer_id] = scatter_grads([(d_low, hidden)])
        d_hidden = jnp.dot(d_low, w_proj_t, preferred_element_type=jnp.float32)
        d_pre = gelu_back(pre_act, d_hidden)
        d_pre_low = d_pre.astype(jnp.bfloat16)
        fc_grads[layer_id] = scatter_grads([(act_two, d_pre_low)])
        fcb_list[layer_id] = jnp.sum(d_pre, axis=0)

        def fc_part(rows, d_pre_low=d_pre_low, w_fc=w_fc):
            return contract_last(d_pre_low[rows], w_fc)

        d_act_two = sum_rows(fc_part, tok_rows)
        normed_two, inv_two = norm_stats(middle)
        d_middle = d_after + norm_back(d_act_two * norm_gain[1], normed_two, inv_two)
        d_mid_low = gather_rows(d_middle.astype(jnp.bfloat16))
        d_mixed = jnp.dot(d_mid_low, w_out_t, preferred_element_type=jnp.float32).astype(
            jnp.bfloat16
        )
        d_queries, d_keys, d_values = attend_back(
            projected[0], projected[1], projected[2], mixed_heads, log_total, d_mixed, allowed
        )
        qv_list[layer_id] = jnp.stack([jnp.sum(d_queries, axis=0), jnp.sum(d_values, axis=0)])
        d_proj_low = jnp.concatenate([d_queries, d_keys, d_values], axis=1).astype(jnp.bfloat16)
        att_grads[layer_id] = scatter_grads([(act_one, d_proj_low), (d_mid_low, mixed_heads)])

        def qkv_part(rows, d_proj_low=d_proj_low, w_qkv=w_qkv):
            return contract_last(d_proj_low[rows], w_qkv)

        d_act_one = sum_rows(qkv_part, tok_rows)
        normed_one, inv_one = norm_stats(residual)
        d_res = d_middle + norm_back(d_act_one * norm_gain[0], normed_one, inv_one)
        gain_list[layer_id] = jnp.stack(
            [jnp.sum(d_act_one * normed_one, axis=0), jnp.sum(d_act_two * normed_two, axis=0)]
        )
        shift_list[layer_id] = jnp.stack(
            [
                jnp.sum(d_act_one, axis=0),
                jnp.sum(d_act_two, axis=0),
                jnp.sum(d_middle, axis=0),
                jnp.sum(d_after, axis=0),
            ]
        )
    qv_rows = jnp.concatenate(qv_list, axis=0)
    small = jnp.concatenate(
        [
            move_columns(jnp.concatenate(gain_list + shift_list, axis=0), matrix, back=True),
            jnp.pad(qv_rows, ((0, 0), (0, width - heads_width))),
            jnp.stack(fcb_list),
        ],
        axis=0,
    )
    small = butterfly_sum(small, "fsdp")
    norm_sum = take_columns(
        butterfly_sum(small[:norm_count], "tp"), gain_cols, device_place * gain_cols
    )
    qv_sum = take_columns(
        small[norm_count : norm_count + 2 * LAYERS, :heads_width], bias_cols, fsdp_place * bias_cols
    )
    fcb_sum = take_columns(small[norm_count + 2 * LAYERS :], unit_cols, fsdp_place * unit_cols)

    def layers_of(grads, columns):
        return [grads[layer][:, columns] for layer in range(LAYERS)]

    rows = fc_weight.shape[1]
    qkv_grad = jnp.stack(
        [
            jnp.transpose(part.reshape(rows, 3, heads_width), (1, 0, 2))
            for part in layers_of(att_grads, slice(0, 3 * heads_width))
        ]
    )
    out_grad = jnp.stack(
        [jnp.transpose(part) for part in layers_of(att_grads, slice(3 * heads_width, None))]
    )
    fc_grad = jnp.stack(fc_grads)
    proj_grad = jnp.stack([jnp.transpose(part) for part in proj_grads])
    return (
        out_rows,
        move_columns(d_res, matrix, back=True),
        qkv_grad,
        qv_sum.reshape(LAYERS, 2, bias_cols),
        out_grad,
        fc_grad,
        fcb_sum,
        proj_grad,
        norm_sum[: 2 * LAYERS].reshape(LAYERS, 2, gain_cols),
        norm_sum[2 * LAYERS :].reshape(LAYERS, 4, gain_cols),
    )


def solution(mesh):
    in_specs = (
        P(("fsdp", "tp"), None),
        P(("fsdp", "tp"), None),
        P("fsdp", None),
        P(None, None, "fsdp", "tp"),
        P(None, None, ("tp", "fsdp")),
        P(None, "tp", "fsdp"),
        P(None, "fsdp", "tp"),
        P(None, ("tp", "fsdp")),
        P(None, "tp", "fsdp"),
        P(None, None, ("fsdp", "tp")),
        P(None, None, ("fsdp", "tp")),
    )
    out_specs = (
        P(("fsdp", "tp"), None),
        P(("fsdp", "tp"), None),
        P(None, None, "fsdp", "tp"),
        P(None, None, ("tp", "fsdp")),
        P(None, "tp", "fsdp"),
        P(None, "fsdp", "tp"),
        P(None, ("tp", "fsdp")),
        P(None, "tp", "fsdp"),
        P(None, None, ("fsdp", "tp")),
        P(None, None, ("fsdp", "tp")),
    )
    return jax.shard_map(body, mesh=mesh, in_specs=in_specs, out_specs=out_specs, check_vma=False)
```
